32 devices in a mesh: pair: 2 (over x), blk: 8 (over z, y), group: 2 (over core).
Axes of the slice: x: 2, y: 2, z: 4, core: 2. Of those that a mesh axis runs over, the one named last changes fastest.
Arguments:
- codes: int32 [32, 1536, 256], P(('pair', 'blk', 'group')), may hold values from 0 to 255
- scales: int32 [32, 1536, 8], P(('pair', 'blk', 'group')), may hold values from -7 to 0
- inputs: bfloat16 [4096, 1536], P(('pair', 'blk', 'group')), may hold values from -6 to 6
- cotangent: bfloat16 [4096, 256], P(('pair', 'blk', 'group')), may hold values from -6 to 6
Outputs:
- earlier_grad: float32 [1536, 256], replicated
- current_grad: float32 [1536, 256], replicated
The draws below stay inside these ranges and needn't reach their ends.
All inputs are finite; a program needn't handle non-finite values.
Results may differ from the reference program's by a relative error of at most 0.0003.
Values sent between devices are 32-bit elements; how exact they have to be, the bound alone decides.
No kernel may reach another device: no remote copies, remote signals or barrier semaphores. Data moves between devices by JAX's collectives and lax.ppermute only.
A program may use at most 64 MiB of HBM per device.

```python
import jax
import jax.numpy as jnp
from jax import lax

D = 1536
KVW = 256
BLOCK = 32
SOURCES = 32
TOKENS = 4096
N_PAIR = 2
N_BLK = 8
N_GROUP = 2


def place_ends(array, stream_key, least, top_value):
    index_at = [jax.random.randint(jax.random.fold_in(stream_key, axis), (), 0, length) for axis, length in enumerate(array.shape)]
    main_axis = array.shape.index(max(array.shape))
    neighbour = index_at[:main_axis] + [(index_at[main_axis] + 1) % array.shape[main_axis]] + index_at[main_axis + 1:]
    return array.at[tuple(index_at)].set(least).at[tuple(neighbour)].set(top_value)


def level_of(rng, extent, pieces, low, high):
    def one(position, blocks):
        draws = jax.random.uniform(jax.random.fold_in(jax.random.fold_in(rng, 6), position), (blocks,), jnp.float32, low / len(pieces), high / len(pieces))
        return jnp.repeat(jnp.exp(draws), extent[position] // blocks).reshape((-1,) + (1,) * (len(extent) - position - 1))

    factor_of = one(*pieces[0])
    for cut in pieces[1:]:
        factor_of = factor_of * one(*cut)
    return factor_of


def gaussian(stream_key, shape, scale, most, pieces=(), dtype=jnp.bfloat16):
    gain = level_of(stream_key, shape, pieces, -0.22, 0.18) if pieces else 1.0
    entries = jax.random.normal(stream_key, shape, jnp.float32) * scale * gain
    return jnp.minimum(jnp.maximum(entries, -most), most).astype(dtype)


def setup_inputs(seed: int = 0) -> dict:
    arg_keys = jax.random.split(jax.random.key(seed), 5)
    codes = place_ends(jax.random.randint(arg_keys[0], (SOURCES, D, KVW), 0, 256), jax.random.fold_in(arg_keys[0], 1), 0, 255).astype(jnp.int32)
    scales = place_ends(jax.random.randint(arg_keys[1], (SOURCES, D, KVW // BLOCK), -7, 1), jax.random.fold_in(arg_keys[1], 1), -7, 0).astype(jnp.int32)
    inputs = gaussian(arg_keys[2], (TOKENS, D), 1.0, 6.0, ((0, 32),))
    cotangent = gaussian(arg_keys[3], (TOKENS, KVW), 1.0, 6.0, ((0, 32),))
    return {"codes": codes, "scales": scales, "inputs": inputs, "cotangent": cotangent}


def decode(codes, scales):
    sign = 1.0 - 2.0 * (codes // 128).astype(jnp.float32)
    field = (codes // 8) % 16
    mant = (codes % 8).astype(jnp.float32)
    frac = jnp.where(field > 0, 8.0 + mant, mant)
    power = jnp.where(field > 0, field, 1) - 10
    expo = power + jnp.repeat(scales, BLOCK, axis=-1)
    return sign * frac * jnp.exp2(expo.astype(jnp.float32))


def reference(codes, scales, inputs, cotangent):
    def accumulate(total, member):
        return total + decode(member[0], member[1]), None

    total, unused = lax.scan(accumulate, jnp.zeros((D, KVW), jnp.float32), (codes, scales))
    count = N_PAIR * N_BLK * N_GROUP
    earlier_grad = total / count
    product = jnp.dot(inputs.T, cotangent, preferred_element_type=jnp.float32)
    current_grad = product / count
    return earlier_grad, current_grad
```

```python
import jax
import jax.numpy as jnp
from jax import lax
from jax.sharding import PartitionSpec as P

AXES = ("pair", "blk", "group")


def decode(codes, scales):
    codes = codes[0]
    scales = scales[0]
    width = codes.shape[1]
    blocks = scales.shape[1]
    unit = jnp.left_shift(1, scales + 7).astype(jnp.float32) * 2.0**-17
    owner = lax.broadcasted_iota(jnp.int32, (blocks, width), 1) // (width // blocks)
    spread = (owner == lax.broadcasted_iota(jnp.int32, (blocks, width), 0)).astype(jnp.float32)
    unit = jnp.dot(unit.astype(jnp.bfloat16), spread.astype(jnp.bfloat16), preferred_element_type=jnp.float32)
    field = (codes >> 3) & 15
    mant = codes & 7
    frac = jnp.where(field > 0, mant + 8, mant)
    whole = jnp.left_shift(frac, jnp.maximum(field, 1)).astype(jnp.float32)
    return jnp.where(codes > 127, -whole, whole) * unit


def key_product(inputs, cotangent):
    return lax.dot_general(
        inputs, cotangent, (((0,), (0,)), ((), ())), preferred_element_type=jnp.float32
    )


def bits_of(size):
    return size.bit_length() - 1


def routes(shape):
    group = [("group", b) for b in range(bits_of(shape["group"]))]
    pair = [("pair", b) for b in range(bits_of(shape["pair"]))]
    blk = [("blk", b) for b in range(bits_of(shape["blk"]))]
    first = pair + blk[:1] + group[1:] + blk[1:]
    second = blk[:1] + pair + group[1:] + blk[1:]
    return group[:1], first, second


def pairs_of(shape, first, second):
    sizes = [shape[a] for a in AXES]
    out = []
    for i in range(sizes[0] * sizes[1] * sizes[2]):
        index = {"group": i % sizes[2], "blk": i // sizes[2] % sizes[1], "pair": i // sizes[2] // sizes[1]}
        axis, bit = first if index["group"] % 2 == 0 else second
        index[axis] ^= 1 << bit
        out.append((i, (index["pair"] * sizes[1] + index["blk"]) * sizes[2] + index["group"]))
    return out


def plan(shape):
    lead, first, second = routes(shape)
    steps = []
    for a, b in [(s, s) for s in lead] + list(zip(first, second)):
        even = lax.axis_index("group") % 2 == 0
        bit_a = (lax.axis_index(a[0]) >> a[1]) & 1
        bit_b = (lax.axis_index(b[0]) >> b[1]) & 1
        steps.append((pairs_of(shape, a, b), bit_a if a == b else jnp.where(even, bit_a, bit_b)))
    return steps


def allsum(part, steps, scale):
    rows = part.shape[0]
    start = 0
    starts = []
    held = part
    for pairs, bit in steps[:-1]:
        half = held.shape[0] // 2
        away = lax.dynamic_slice_in_dim(held, (1 - bit) * half, half, 0)
        keep = lax.dynamic_slice_in_dim(held, bit * half, half, 0)
        starts.append(start)
        start = start + bit * half
        held = keep + lax.ppermute(away, AXES, pairs)
    pairs, bit = steps[-1]
    held = (held + lax.ppermute(held, AXES, pairs)) * scale
    for pairs, bit in reversed(steps[:-1]):
        other = lax.ppermute(held, AXES, pairs)
        held = jnp.where(bit == 0, jnp.concatenate([held, other]), jnp.concatenate([other, held]))
    return held


def make(shape):
    def local(codes, scales, inputs, cotangent):
        count = shape["pair"] * shape["blk"] * shape["group"]
        steps = plan(shape)
        product = key_product(inputs, cotangent)
        current_grad = allsum(product, steps, 1.0 / count)
        decoded = decode(codes, scales)
        earlier_grad = allsum(decoded, steps, 1.0 / count)
        return (earlier_grad, current_grad)

    return local


def solution(mesh):
    in_specs = (
        P(("pair", "blk", "group"), None, None),
        P(("pair", "blk", "group"), None, None),
        P(("pair", "blk", "group"), None),
        P(("pair", "blk", "group"), None),
    )
    out_specs = (P(), P())
    return jax.shard_map(make(dict(mesh.shape)), mesh=mesh, in_specs=in_specs, out_specs=out_specs, check_vma=False)
```

```python
import functools

import jax
import jax.numpy as jnp
from jax import lax
from jax.experimental import pallas as pl
from jax.experimental.pallas import tpu as pltpu
from jax.sharding import PartitionSpec as P


AXES = ("pair", "blk", "group")
CHUNKS = (((0, 0, 8),), ((0, 8, 12), (1, 0, 4)), ((1, 4, 12),))
PARTS = 12
ROUTES = (
    ((0, 2, 1, 3), (1, 0, 2, 3)),
    ((1, 2, 0, 3), (2, 0, 3, 1)),
    ((2, 1, 0, 3), (0, 2, 1, 3)),
)
SUBLANES = 8
VMEM = pl.BlockSpec(memory_space=pltpu.VMEM)
HBM = pl.BlockSpec(memory_space=pltpu.HBM)
GRANT = 8 * 1024 * 1024


def bits_of(size):
    return size.bit_length() - 1


def routes(shape, order):
    group = [("group", b) for b in range(bits_of(shape["group"]))]
    bits = [(axis, b) for axis in ("pair", "blk") for b in range(bits_of(shape[axis]))] + group[1:]
    both = [[bits[k] for k in one if k < len(bits)] + bits[len(one):] for one in order]
    return [(group[0], group[0])] + list(zip(*both))


def side_of(shape, index):
    total = 0
    for axis in AXES:
        for b in range(bits_of(shape[axis])):
            total = total + ((index[axis] >> b) & 1)
    return total % 2


def pairs_of(shape, route, first):
    sizes = [shape[a] for a in AXES]
    out = []
    for i in range(sizes[0] * sizes[1] * sizes[2]):
        index = {"group": i % sizes[2], "blk": i // sizes[2] % sizes[1], "pair": i // sizes[2] // sizes[1]}
        axis, bit = route[side_of(shape, index)]
        index[axis] ^= 1 << bit
        if not first:
            index["group"] ^= 1
        out.append((i, (index["pair"] * sizes[1] + index["blk"]) * sizes[2] + index["group"]))
    return out


def side_now(shape):
    return side_of(shape, {axis: lax.axis_index(axis) for axis in AXES})


def bit_now(shape, route):
    values = [(lax.axis_index(axis) >> bit) & 1 for axis, bit in route]
    if route[0] == route[1]:
        return values[0]
    return jnp.where(side_now(shape) == 0, values[0], values[1])


def call(body, outs, *args, hbm_in=(), hbm_out=False, alias=None, scratch=()):
    ins = [HBM if i in hbm_in else VMEM for i in range(len(args))]
    args = [pltpu.with_memory_space_constraint(a, pltpu.HBM if i in hbm_in else pltpu.VMEM) for i, a in enumerate(args)]
    make_out, spec = (pltpu.HBM, HBM) if hbm_out else (pltpu.VMEM, VMEM)
    return list(pl.pallas_call(
        body, out_shape=[make_out(s, d) for s, d in outs], in_specs=ins, out_specs=[spec] * len(outs),
        scratch_shapes=list(scratch), input_output_aliases=alias or {},
        compiler_params=pltpu.CompilerParams(vmem_limit_bytes=GRANT),
    )(*args))


def aligned(start, size, to=SUBLANES):
    return pl.ds(pl.multiple_of(start, to), size)


def product_body(shape, plan, x_hbm, c_hbm, codes_hbm, scales_hbm, *refs):
    n = len(refs) - 5
    results, codes_ref, scales_ref = refs[:n], refs[n], refs[n + 1]
    x_ref, c_ref, sem = refs[n + 2:]
    copies = [pltpu.make_async_copy(a, b, sem.at[k]) for k, (a, b) in enumerate(
        ((x_hbm, x_ref), (c_hbm, c_ref), (scales_hbm, scales_ref), (codes_hbm, codes_ref)))]
    for copy in copies:
        copy.start()
    copies[0].wait()
    copies[1].wait()
    side = side_now(shape)
    half = x_ref.shape[1] // 2
    for k, to, start, rows in plan:
        for ref, of in ((results[2 * k], 1 - side), (results[2 * k + 1], side)):
            ref[pl.ds(to, rows), :] = lax.dot_general(
                x_ref[:, aligned(of * half + start, rows, 128)], c_ref[...], (((0,), (0,)), ((), ())),
                preferred_element_type=jnp.float32)
    copies[2].wait()
    copies[3].wait()


def decode_body(shape, plan, codes_ref, scales_ref, *refs):
    away_ref, keep_ref = refs[-2:]
    side = side_now(shape)
    height, width = codes_ref.shape
    blocks = scales_ref.shape[0]
    owner = lax.broadcasted_iota(jnp.int32, (blocks, width), 1) // (width // blocks)
    spread = (owner == lax.broadcasted_iota(jnp.int32, (blocks, width), 0)).astype(jnp.float32).astype(jnp.bfloat16)
    for to, start, rows in plan:
        for ref, of in ((away_ref, 1 - side), (keep_ref, side)):
            first = of * (height // 2) + start
            unit = jnp.left_shift(1, scales_ref[:, aligned(first, rows, 128)] + 7).astype(jnp.float32) * 2.0**-17
            unit = lax.dot_general(
                unit.astype(jnp.bfloat16), spread, (((0,), (0,)), ((), ())), preferred_element_type=jnp.float32)
            codes = codes_ref[aligned(first, rows), :]
            field = (codes >> 3) & 15
            mant = codes & 7
            frac = jnp.where(field > 0, mant + 8, mant)
            whole = jnp.left_shift(frac, jnp.maximum(field, 1)).astype(jnp.float32)
            ref[pl.ds(to, rows), :] = jnp.where(codes > 127, -whole, whole) * unit


def split_body(shape, route, keep_ref, got_ref, away_ref, held_ref):
    half = away_ref.shape[0]
    bit = bit_now(shape, route)
    for ref, of in ((away_ref, 1 - bit), (held_ref, bit)):
        rows = aligned(of * half, half)
        ref[...] = keep_ref[rows, :] + got_ref[rows, :]


def add_body(scale, keep_ref, got_ref, out_ref):
    out_ref[...] = (keep_ref[...] + got_ref[...]) * scale


def join_body(shape, route, held_ref, got_ref, out_ref):
    half = held_ref.shape[0]
    bit = bit_now(shape, route)
    for ref, of in ((held_ref, bit), (got_ref, 1 - bit)):
        out_ref[aligned(of * half, half), :] = ref[...]


def write_body(shape, plan, n_out, *refs):
    outs, sem = refs[-n_out - 1:-1], refs[-1]
    side = side_now(shape)
    copies = []
    for k, (i, at, o, start, rows, other) in enumerate(plan):
        of = 1 - side if other else side
        to = outs[o].at[aligned(of * (outs[o].shape[0] // 2) + start, rows), :]
        copies.append(pltpu.make_async_copy(refs[i].at[pl.ds(at, rows), :], to, sem.at[k]))
        copies[-1].start()
    for copy in copies:
        copy.wait()


class Chunk:
    def __init__(self, shape, order):
        self.shape = shape
        self.steps = routes(shape, order)
        self.pairs = [pairs_of(shape, s, i == 0) for i, s in enumerate(self.steps)]
        self.scale = 1.0 / (shape["pair"] * shape["blk"] * shape["group"])
        self.undo = []
        self.turned = False

    def begin(self, away, keep):
        self.keep = keep
        self.send(away, 0)

    def send(self, x, step):
        self.got = lax.ppermute(x, AXES, self.pairs[step])
        self.step = step

    def one(self, body, keep):
        (out,) = call(body, [(keep, jnp.float32)], self.keep, self.got)
        return out

    def go(self):
        last = len(self.steps) - 1
        rows, width = self.keep.shape
        shape = self.shape
        if self.step < last and not self.turned:
            i = self.step + 1
            half = rows // 2
            if i < last and half % SUBLANES == 0:
                away, self.keep = call(functools.partial(split_body, shape, self.steps[i]),
                                       [((half, width), jnp.float32)] * 2, self.keep, self.got)
                self.undo.append(i)
                self.send(away, i)
            else:
                self.keep = self.one(functools.partial(add_body, 1.0), (rows, width))
                self.send(self.keep, i)
        elif not self.turned:
            self.keep = self.one(functools.partial(add_body, self.scale), (rows, width))
            self.turned = True
            self.send(self.keep, self.undo[-1] if self.undo else 0)
        else:
            i = self.undo.pop()
            self.keep = self.one(functools.partial(join_body, shape, self.steps[i]), (2 * rows, width))
            self.send(self.keep, self.undo[-1] if self.undo else 0)

    def ended(self):
        return self.turned and not self.undo


def make(shape):
    def local(codes, scales, inputs, cotangent):
        height, width = codes.shape[1:]
        half = height // 2
        f32 = jnp.float32
        jobs = []
        for pieces in CHUNKS:
            at = 0
            job = []
            for o, start, end in pieces:
                start, end = half * start // PARTS, half * end // PARTS
                job.append((o, at, start, end - start))
                at += end - start
            jobs.append((job, at))
        plan, outs, first = [], [], {}
        for c, (job, rows) in enumerate(jobs):
            for o, at, start, size in job:
                if o == 0:
                    if c not in first:
                        first[c] = len(outs) // 2
                        outs += [((rows, width), f32)] * 2
                    plan.append((first[c], at, start, size))
        flat, scale_rows = codes[0], scales[0].T
        vm = [((height, width), jnp.int32), (scale_rows.shape, jnp.int32)]
        got = call(functools.partial(product_body, shape, plan), outs + vm, inputs, cotangent, flat, scale_rows,
                   hbm_in=(0, 1, 2, 3),
                   scratch=[pltpu.VMEM(inputs.shape, inputs.dtype), pltpu.VMEM(cotangent.shape, cotangent.dtype),
                            pltpu.SemaphoreType.DMA((4,))])
        flat, scale_rows = got[-2:]
        chains = []
        for c, (job, rows) in enumerate(jobs):
            pair = got[2 * first[c]:2 * first[c] + 2] if c in first else []
            plan = [(at, start, size) for o, at, start, size in job if o == 1]
            if plan:
                pair = call(functools.partial(decode_body, shape, plan), [((rows, width), f32)] * 2,
                            flat, scale_rows, *pair, alias={2: 0, 3: 1} if pair else None)
            chain = Chunk(shape, ROUTES[c])
            chain.begin(*pair)
            chains.append(chain)
        while not all(chain.ended() for chain in chains):
            for chain in chains:
                if not chain.ended():
                    chain.go()
        ins = [chain.keep for chain in chains] + [chain.got for chain in chains]
        n = len(chains)
        plan = [(c + n * other, at, o, start, size, other)
                for other in (0, 1) for c, (job, _) in enumerate(jobs) for o, at, start, size in job]
        full = ((height, width), f32)
        outs = []
        for other in (0, 1):
            part = [(i - n * other, *rest) for i, *rest in plan if rest[-1] == other]
            outs = call(functools.partial(write_body, shape, part, 2), [full] * 2, *ins[n * other:n * other + n],
                        *outs, hbm_in=(n, n + 1), hbm_out=True, alias={n: 0, n + 1: 1} if outs else None,
                        scratch=[pltpu.SemaphoreType.DMA((len(part),))])
        return (outs[1], outs[0])

    return local


def solution(mesh):
    in_specs = (
        P(("pair", "blk", "group"), None, None),
        P(("pair", "blk", "group"), None, None),
        P(("pair", "blk", "group"), None),
        P(("pair", "blk", "group"), None),
    )
    out_specs = (P(), P())
    return jax.shard_map(make(dict(mesh.shape)), mesh=mesh, in_specs=in_specs, out_specs=out_specs, check_vma=False)
```
